256 devices in a mesh: box: 64 (over x, z, core), col: 4 (over y).
Axes of the slice: x: 4, y: 4, z: 8, core: 2. Of those that a mesh axis runs over, the one named last changes fastest.
Arguments:
- leaf_maps: float32 [64, 1024, 1024], P('box', None, 'col'), as said below
- leaf_nodes: int32 [64, 4, 256], P('box'), may hold values from 0 to 255, each once within a row
Outputs:
- top_maps: float32 [64, 1024, 1024], P('box', None, 'col')
The draws below stay inside these ranges and needn't reach their ends.
Inputs may be any that keep to these rules, and one draw needn't show every extreme that they name: `leaf_maps`: each leaf map is symmetric and positive definite. `leaf_nodes`: for each leaf and side, the entries are a permutation of 0 to 255.
All inputs are finite; a program needn't handle non-finite values.
Results may differ from the reference program's by a relative error of at most 0.0003.
Values sent between devices are 32-bit elements; how exact they have to be, the bound alone decides.
No kernel may reach another device: no remote copies, remote signals or barrier semaphores. Data moves between devices by JAX's collectives and lax.ppermute only.
A program may use at most 64 MiB of HBM per device.

```python
import jax
import jax.numpy as jnp
from jax import lax

Q = 256
BOXES = 64


def draw_leaf_maps(key, part):
    width_all = 4 * Q
    basis_key = jax.random.fold_in(key, 11)
    coin_key = jax.random.fold_in(key, 23)
    small_key = jax.random.fold_in(key, 37)
    large_key = jax.random.fold_in(key, 41)
    mixing_key = jax.random.fold_in(key, 53)
    raw_basis = jax.random.normal(basis_key, (BOXES, 4, Q, Q), jnp.float32)
    basis, upper = jnp.linalg.qr(raw_basis)
    coin = jax.random.uniform(coin_key, (BOXES, 4, Q), jnp.float32)
    small_levels = jnp.exp(jax.random.uniform(small_key, (BOXES, 4, Q), jnp.float32, -6.0, -3.0))
    large_levels = jnp.exp(jax.random.uniform(large_key, (BOXES, 4, Q), jnp.float32, -1.0, 1.5))
    levels = jnp.where(coin < 0.8, small_levels, large_levels)
    mixing = jax.random.normal(mixing_key, (BOXES, 4, Q, Q), jnp.float32) * Q ** (-0.5)
    scales = jnp.ones((BOXES, width_all), jnp.float32)
    spread = (jnp.sqrt(levels)[..., None] * mixing).reshape(BOXES, width_all, Q)
    inner = 0.6 * jnp.einsum('bik,bjk->bij', spread, spread, precision=lax.Precision.HIGHEST)
    inner = inner + 0.4 * jnp.eye(width_all, dtype=jnp.float32)[None] * levels.reshape(BOXES, width_all)[:, None, :]
    blocked = inner.reshape(BOXES, 4, Q, 4, Q)
    left = jnp.einsum('bsij,bsjul->bsiul', basis, blocked, precision=lax.Precision.HIGHEST)
    full = jnp.einsum('bsiul,bukl->bsiuk', left, basis, precision=lax.Precision.HIGHEST)
    leaf_block = full.reshape(BOXES, width_all, width_all)
    leaf_block = 0.5 * (leaf_block + jnp.swapaxes(leaf_block, 1, 2))
    return leaf_block * scales[:, :, None] * scales[:, None, :]


def setup_inputs(seed: int = 0) -> dict:
    key_list = jax.random.split(jax.random.key(seed), 3)
    return {
        "leaf_maps": draw_leaf_maps(jax.random.fold_in(key_list[2], 71), 0),
        "leaf_nodes": jax.vmap(lambda own: jax.random.permutation(own, Q))(jax.random.split(key_list[1], BOXES * 4)).reshape((BOXES, 4, Q)).astype(jnp.int32),
    }


PANEL_TABLE = ((0, 2, 4, 6), (1, 2, 5, 6), (0, 3, 4, 7), (1, 3, 5, 7))
HALF_TABLE = ((0, 1, 1, 0), (0, 0, 1, 1), (1, 1, 0, 0), (1, 0, 0, 1))

def cholesky_apply(coupling, right_side):
    factor = jnp.linalg.cholesky(coupling)
    forward = lax.linalg.triangular_solve(factor, right_side, left_side=True, lower=True)
    return lax.linalg.triangular_solve(factor, forward, left_side=True, lower=True, transpose_a=True)

def canonical_map(leaf_block, side_nodes):
    bases = (jnp.arange(4, dtype=jnp.int32) * Q)[:, None]
    row_order = (bases + side_nodes).reshape(-1).astype(jnp.int32)
    return jnp.take(jnp.take(leaf_block, row_order, axis=0), row_order, axis=1)

def merge_maps(first_map, second_map, first_iface, second_iface, block_order):
    children = (first_map, second_map)
    ifaces = (first_iface, second_iface)
    coupling = first_map[first_iface, first_iface] + second_map[second_iface, second_iface]
    upper_rows = jnp.concatenate([children[child][start:start + length, ifaces[child]] for child, start, length in block_order], axis=0)
    right_side = jnp.concatenate([children[child][ifaces[child], start:start + length] for child, start, length in block_order], axis=1)
    row_blocks = []
    for row_child, row_start, row_len in block_order:
        pieces = []
        for col_child, col_start, col_len in block_order:
            if row_child == col_child:
                pieces.append(children[row_child][row_start:row_start + row_len, col_start:col_start + col_len])
            else:
                pieces.append(jnp.zeros((row_len, col_len), jnp.float32))
        row_blocks.append(jnp.concatenate(pieces, axis=1))
    diagonal_part = jnp.concatenate(row_blocks, axis=0)
    solved = cholesky_apply(coupling, right_side)
    return diagonal_part - jnp.dot(upper_rows.astype(jnp.float32), solved.astype(jnp.float32), precision=lax.Precision.HIGHEST, preferred_element_type=jnp.float32)

def top_box(maps_four, nodes_four):
    leaves = [canonical_map(maps_four[index], nodes_four[index]) for index in range(4)]
    first_order = [(0, 0, Q), (1, 0, Q), (1, Q, Q), (0, 2 * Q, Q), (1, 2 * Q, Q), (0, 3 * Q, Q)]
    lower_pair = merge_maps(leaves[0], leaves[1], slice(Q, 2 * Q), slice(3 * Q, 4 * Q), first_order)
    upper_pair = merge_maps(leaves[2], leaves[3], slice(Q, 2 * Q), slice(3 * Q, 4 * Q), first_order)
    second_order = [(0, 0, 2 * Q), (0, 2 * Q, Q), (1, 2 * Q, Q), (1, 3 * Q, 2 * Q), (0, 5 * Q, Q), (1, 5 * Q, Q)]
    whole = merge_maps(lower_pair, upper_pair, slice(3 * Q, 5 * Q), slice(0, 2 * Q), second_order)
    outputs = []
    for quarter in range(4):
        pieces = []
        for column in range(4):
            panel_id = PANEL_TABLE[quarter][column]
            half_id = HALF_TABLE[quarter][column]
            pieces.append(whole[half_id * 4 * Q:(half_id + 1) * 4 * Q, panel_id * Q:(panel_id + 1) * Q])
        outputs.append(jnp.concatenate(pieces, axis=1))
    return jnp.stack(outputs)

def reference(leaf_maps, leaf_nodes):
    grouped_maps = leaf_maps.reshape(BOXES // 4, 4, 4 * Q, 4 * Q)
    grouped_nodes = leaf_nodes.reshape(BOXES // 4, 4, 4, Q)
    result = lax.map(lambda pair_args: top_box(pair_args[0], pair_args[1]), (grouped_maps, grouped_nodes))
    return result.reshape(BOXES, 4 * Q, 4 * Q)
```

```python
import jax
import jax.numpy as jnp
from jax import lax
from jax.experimental import pallas as pl
from jax.experimental.pallas import tpu as pltpu
from jax.sharding import PartitionSpec as P

Q = 256
F32 = jnp.float32
BF16 = jnp.bfloat16
HIGHEST = lax.Precision.HIGHEST
VMEM = pl.BlockSpec(memory_space=pltpu.VMEM)
SMEM = pl.BlockSpec(memory_space=pltpu.SMEM)
ANY = pl.BlockSpec(memory_space=pl.ANY)


def dot(a, b):
    return jnp.dot(a, b, precision=HIGHEST, preferred_element_type=F32)


def dot_t(a, b):
    return lax.dot_general(
        a, b, (((1,), (1,)), ((), ())), precision=HIGHEST, preferred_element_type=F32
    )


def row_of(x, j):
    return jnp.broadcast_to(x[j : j + 1, :], (8, 128))


def col_of(x, j):
    return jnp.broadcast_to(x[:, j : j + 1], (8, 128))


def eliminate(rows, tile, base, lane, sub):
    cols = [col_of(rows[tile], base + j) for j in range(8)]
    rows = list(rows)
    for j in range(0, 8, 2):
        c0, c1 = cols[j], cols[j + 1]
        a, b2 = row_of(c0, j), row_of(c1, j)
        b, c = row_of(c0, j + 1), row_of(c1, j + 1)
        rd = 1.0 / (a * c - b * b2)
        l0, l1 = lane == base + j, lane == base + j + 1
        s0, s1 = sub == j, sub == j + 1

        def scaled(x):
            r0, r1 = row_of(x, j), row_of(x, j + 1)
            return (c * r0 - b2 * r1) * rd, (a * r1 - b * r0) * rd

        def put(old, n0, n1):
            return jnp.where(s0, n0, jnp.where(s1, n1, old - (c0 * n0 + c1 * n1)))

        for m in range(j + 2, 8):
            cols[m] = put(cols[m], *scaled(cols[m]))
        for i in range(len(rows)):
            n0, n1 = scaled(rows[i])
            old = rows[i]
            if i == tile:
                n0 = jnp.where(l0, c * rd, jnp.where(l1, -(b2 * rd), n0))
                n1 = jnp.where(l0, -(b * rd), jnp.where(l1, a * rd, n1))
                old = jnp.where(l0 | l1, 0.0, old)
            rows[i] = put(old, n0, n1)
    return rows


def update(rows, pivots, tile, base, in_block):
    cols = [col_of(rows[tile], base + j) for j in range(8)]
    out = []
    for i in range(len(rows)):
        x = jnp.where(in_block, 0.0, rows[i]) if i == tile else rows[i]
        p = [cols[j] * pivots[i][j] for j in range(8)]
        out.append(x - (((p[0] + p[1]) + (p[2] + p[3])) + ((p[4] + p[5]) + (p[6] + p[7]))))
    return out


def invert(A, w=32):
    n = A.shape[0]
    tiles, groups_in = n // 128, w // 8
    lane = lax.broadcasted_iota(jnp.int32, (8, 128), 1)
    sub = lax.broadcasted_iota(jnp.int32, (8, 128), 0)
    wide = lax.broadcasted_iota(jnp.int32, (1, n), 1)
    panel = A[0:w, :]
    for r0 in range(0, n, w):
        tile, b0 = r0 // 128, r0 % 128
        groups = [
            [panel[g * 8 : g * 8 + 8, i * 128 : i * 128 + 128] for i in range(tiles)]
            for g in range(groups_in)
        ]
        for b in range(groups_in):
            base = b0 + b * 8
            in_block = (lane >= base) & (lane < base + 8)
            done = eliminate(groups[b], tile, base, lane, sub)
            pivots = [[row_of(done[i], j) for j in range(8)] for i in range(tiles)]
            groups[b] = done
            for g in list(range(b + 1, groups_in)) + list(range(b)):
                groups[g] = update(groups[g], pivots, tile, base, in_block)
        final = jnp.concatenate([jnp.concatenate(g, axis=1) for g in groups], axis=0)
        in_panel = (wide >= r0) & (wide < r0 + w)

        def trail(lo, hi):
            x = A[lo:hi, :]
            return jnp.where(in_panel, 0.0, x) - dot(x[:, r0 : r0 + w], final)

        nxt = r0 + w
        if nxt < n:
            panel = trail(nxt, nxt + w)
            if nxt + w < n:
                A[nxt + w : n, :] = trail(nxt + w, n)
        if r0 > 0:
            A[0:r0, :] = trail(0, r0)
        A[r0:nxt, :] = final


def call(kernel, out_shape, in_specs, flops, scratch=(), name=None, limit=None):
    outs = [jax.ShapeDtypeStruct(s, F32) for s in out_shape]
    return pl.pallas_call(
        kernel,
        out_shape=outs,
        in_specs=in_specs,
        out_specs=[VMEM] * len(outs),
        scratch_shapes=list(scratch),
        cost_estimate=pl.CostEstimate(flops=flops, bytes_accessed=1 << 20, transcendentals=0),
        compiler_params=pltpu.CompilerParams(vmem_limit_bytes=limit or (40 << 20)),
        name=name,
    )


def permute_kernel(role, panel, nodes, s_out, u_out, c_out, d_out):
    own = role[0]
    sides = [role[1], role[2], role[3], role[4]]
    picks = [nodes[pl.ds(s, 1), :] for s in sides] + [nodes[pl.ds(own, 1), :]]
    table = jnp.concatenate(picks + [jnp.zeros((3, Q), jnp.int32)], axis=0).T
    lanes = lax.broadcasted_iota(jnp.int32, (Q, Q), 1)

    def one_hot(k):
        return jnp.where(lanes == jnp.broadcast_to(table[:, k : k + 1], (Q, Q)), 1.0, 0.0).astype(BF16)

    def mul(a, b):
        return jnp.dot(a, b, preferred_element_type=F32)

    def mul_t(a, b):
        return lax.dot_general(a, b, (((1,), (1,)), ((), ())), preferred_element_type=F32)

    to_own = one_hot(4)
    for k in range(4):
        x = panel[pl.ds(pl.multiple_of(sides[k] * Q, Q), Q), :]
        x1 = x.astype(BF16)
        rest = x - x1.astype(F32)
        x2 = rest.astype(BF16)
        x3 = (rest - x2.astype(F32)).astype(BF16)
        hot = one_hot(k)
        parts = [mul(hot, piece).astype(BF16) for piece in (x1, x2, x3)]
        if k < 2:
            flipped = [mul_t(to_own, piece) for piece in parts]
            value = flipped[0] + (flipped[1] + flipped[2])
            u_out[:, k * Q : k * Q + Q] = value
            if k == 0:
                s_out[...] = value
        if k > 0:
            straight = [mul_t(piece, to_own) for piece in parts]
            value = straight[0] + (straight[1] + straight[2])
            if k == 1:
                c_out[...] = value
            else:
                d_out[(k - 2) * Q : (k - 1) * Q, :] = value


def first_inverse_kernel(s_own, s_peer, inv):
    inv[...] = s_own[...] + s_peer[...]
    invert(inv)


def level_one_kernel(role, inv, own, peer, zt, c00, mine, c01, c11):
    west = role[5] == 0
    a, b = own[...], peer[...]
    kn_w, kn_e = jnp.where(west, a, b), jnp.where(west, b, a)
    k_w, n_w, k_e, n_e = kn_w[:Q], kn_w[Q:], kn_e[:Q], kn_e[Q:]
    z_w, z_e = dot(k_w, inv[...]), dot(k_e, inv[...])
    zt[:Q, :] = z_w
    zt[Q:, :] = z_e
    c00[...] = n_w - dot_t(z_w, k_w)
    we = -dot_t(z_w, k_e)
    ee = n_e - dot_t(z_e, k_e)
    c01[...] = we
    c11[...] = ee
    mine[:Q, :] = jnp.where(west, we, ee)
    mine[Q:, :] = jnp.where(west, z_w, z_e)


def second_inverse_kernel(c_own, c_peer, inv):
    inv[...] = c_own[...] + c_peer[...]
    invert(inv)


def third_inverse_kernel(role, inv0, c01, c11, far, far_peer, gt, b_out, inv):
    west = role[5] == 0
    f, g = far[...], far_peer[...]
    b = c01[...] + jnp.where(west, f, g)
    d = c11[...] + jnp.where(west, g, f)
    b_out[...] = b
    gt[...] = dot(b.T, inv0[...])
    inv[...] = d - dot(gt[...], b)
    invert(inv)


def final_kernel(
    role, inv_own, inv_far, zt_own, zt_far, zt_far_peer, inv0, b, gt, inv1,
    d_own, d_far, e0, e1, e2, e3, w0, w1, w2, w3, out, ux, up, x, t, zf, sem,
):
    own, core, zpos, ext = role[0], role[5], role[6], role[7]
    half = 1 - ext
    even = 1 - own % 2
    near, far = (1 - ext) * (1 - even), (1 - ext) * even
    mine, theirs = (e0, e1, e2, e3), (w0, w1, w2, w3)
    p_copy = pltpu.make_async_copy(e0, up, sem.at[4])
    for use, ref in ((near == 0, e0), (near == 1, w0)):
        @pl.when(use)
        def _(ref=ref):
            pltpu.make_async_copy(ref, up, sem.at[4]).start()
    for j in range(2):
        col = 2 * half + j
        shift = (own - col + 4) % 4
        flip = jnp.where(col == 1, (zpos + 1 - core) % 2, jnp.where(col == 3, (zpos + core) % 2, core))
        for i in range(4):
            @pl.when(shift == i)
            def _(i=i, j=j, flip=flip):
                pltpu.make_async_copy(mine[i], ux.at[2 * j + flip], sem.at[2 * j]).start()
                pltpu.make_async_copy(theirs[i], ux.at[2 * j + 1 - flip], sem.at[2 * j + 1]).start()
    west = core == 0
    zf[:Q, :] = jnp.where(west, zt_far[...], zt_far_peer[...])
    zf[Q:, :] = jnp.where(west, zt_far_peer[...], zt_far[...])
    p_copy.wait()
    is_far = far == 1
    a_p, c_p = up[:, :Q], up[:, Q:]
    inv_p = jnp.where(is_far, inv_far[...], inv_own[...])
    zt_p = jnp.where(is_far, zf[...], zt_own[...])
    p_core = jnp.where(near == 1, 1 - core, core)
    p_zpos = jnp.where(is_far, 1 - zpos, zpos)
    y = dot(a_p, inv_p)
    v2 = -dot_t(a_p, zt_p)
    on_west = p_core == 0
    v2_w = v2[:, :Q] + jnp.where(on_west, c_p, 0.0)
    v2_e = v2[:, Q:] + jnp.where(on_west, 0.0, c_p)
    u1 = dot(v2_w, inv0[...])
    s2 = dot(v2_e - dot(u1, b[...]), inv1[...])
    s1 = u1 - dot(s2, gt[...])
    x[:, :Q] = s1
    x[:, Q:] = s2
    xs = x[...]
    own_t = dot(xs, zt_own[...])
    far_t = dot(xs, zf[...])
    t[0] = jnp.where(is_far, -own_t, y - own_t)
    t[1] = jnp.where(is_far, y - far_t, -far_t)
    for j in range(4):
        pltpu.make_async_copy(e0, ux.at[j], sem.at[j]).wait()
    pairs = ((0, 1), (0, 1), (0, 0), (1, 1))
    leaves = ((0, 0), (1, 1), (1, 0), (1, 0))
    for k in range(4):
        pair = jnp.where(half == 0, pairs[k][0], pairs[k][1])
        leaf = jnp.where(half == 0, leaves[k][0], leaves[k][1])
        tk = t[jnp.where(pair == zpos, 0, 1)]
        xk = jnp.where(leaf == 0, x[:, :Q], x[:, Q:])
        out[k * Q : k * Q + Q, :] = -(dot_t(ux[k, :, :Q], tk) + dot_t(ux[k, :, Q:], xk))
    z_row = pl.ds(pl.multiple_of(p_core * Q, Q), Q)
    x_row = pl.ds(pl.multiple_of((2 + p_zpos) * Q, Q), Q)
    for use, ref in ((ext == 1, d_own), (ext == 0, d_far)):
        @pl.when(use & (half == 1 - p_core))
        def _(ref=ref):
            out[x_row, :] = out[x_row, :] + ref[:Q, :]

        @pl.when(use & (half == p_zpos))
        def _(ref=ref):
            out[z_row, :] = out[z_row, :] + ref[Q:, :]


def sides_of(core, zpos):
    return 1 + 2 * core, 2 - 2 * zpos, 3 - 2 * core, 2 * zpos


def pairs_of(boxes, route):
    out = []
    for k in range(boxes // 4):
        for z in range(2):
            for core in range(2):
                for col in range(4):
                    to = route(core, z, col)
                    if to is not None:
                        out.append((
                            (4 * k + 2 * z + core) * 4 + col,
                            (4 * k + 2 * to[1] + to[0]) * 4 + to[2],
                        ))
    return out


def shards(leaf_maps, leaf_nodes):
    boxes = lax.axis_size("box")

    def send(value, route):
        return lax.ppermute(value, ("box", "col"), pairs_of(boxes, route))

    def swap_core(core, z, col):
        return 1 - core, z, col

    def swap_z(core, z, col):
        return core, 1 - z, col

    def is_ext(core, z, col):
        return col in sides_of(core, z)[2:]

    def shift_if(test, step):
        return lambda core, z, col: (core, z, (col + step) % 4) if test(core, z, col) else None

    box = lax.axis_index("box")
    col = lax.axis_index("col")
    core, zpos = box % 2, box // 2 % 2
    ia, ic, ex, ez = sides_of(core, zpos)
    ext = ((col == ex) | (col == ez)).astype(jnp.int32)
    role = jnp.stack([col, ia, ic, ex, ez, core, zpos, ext]).astype(jnp.int32)

    square = (Q, Q)
    s_part, u_part, c_part, d_part = call(
        permute_kernel, [square, (Q, 2 * Q), square, (2 * Q, Q)], [SMEM, VMEM, VMEM], 1 << 30, name="permute"
    )(role, leaf_maps[0], leaf_nodes[0])

    def from_ia(core, z, col):
        return col == sides_of(core, z)[0]

    got = [send(s_part, shift_if(from_ia, s)) for s in (1, 2, 3)]
    s_own = jnp.where(col == ia, s_part, got[0] + got[1] + got[2])
    s_peer = send(s_own, swap_core)

    def from_inner(core, z, col):
        return col in sides_of(core, z)[:2]

    got = [c_part] + [send(c_part, shift_if(from_inner, s)) for s in (1, 2, 3)]

    def pick(side):
        shift = (col - side + 4) % 4
        return jnp.where(shift == 0, got[0], jnp.where(shift == 1, got[1], jnp.where(shift == 2, got[2], got[3])))

    kn_own = jnp.concatenate([pick(ia), pick(ic)], axis=0)
    kn_peer = send(kn_own, swap_core)

    def spread(core, z, col):
        if not is_ext(core, z, col):
            return None
        return (core, 1 - z, col) if col % 2 == 0 else (1 - core, 1 - z, col)

    e0 = jnp.where(ext == 1, u_part, send(u_part, spread))

    def wanted(step):
        def route(core, z, col):
            to = (col + step) % 4
            if to == 0 and (col in (0, 1)) == (z == 1):
                return None
            if to == 2 and (col in (0, 1)) == (z == 0):
                return None
            return core, z, to
        return route

    ring = [e0] + [send(e0, wanted(s)) for s in (1, 2, 3)]
    ring_peer = [send(v, swap_core) for v in ring]

    def to_inner(core, z, col):
        if not is_ext(core, z, col):
            return None
        return (core, 1 - z, col) if col % 2 == 0 else (1 - core, z, col)

    d_far = send(d_part, to_inner)

    inv_own, = call(first_inverse_kernel, [square], [VMEM] * 2, 10 << 30, name="first_inverse")(s_own, s_peer)
    zt, c00, mine, c01, c11 = call(
        level_one_kernel,
        [(2 * Q, Q), square, (2 * Q, Q), square, square],
        [SMEM] + [VMEM] * 3,
        2 << 30,
        name="level_one",
    )(role, inv_own, kn_own, kn_peer)

    c00_far = send(c00, swap_z)
    mine_far = send(mine, swap_z)
    mine_far_peer = send(mine_far, swap_core)

    def to_far_inner(core, z, col):
        return (core, 1 - z, col) if is_ext(core, z, col) and col % 2 == 0 else None

    inv_far = send(inv_own, to_far_inner)

    inv0, = call(second_inverse_kernel, [square], [VMEM] * 2, 10 << 30, name="second_inverse")(c00, c00_far)
    gt, b, inv1 = call(
        third_inverse_kernel, [square] * 3, [SMEM] + [VMEM] * 5, 10 << 30, name="third_inverse"
    )(role, inv0, c01, c11, mine_far[:Q], mine_far_peer[:Q])
    out, = call(
        final_kernel,
        [(4 * Q, Q)],
        [SMEM] + [VMEM] * 11 + [ANY] * 8,
        4 << 30,
        scratch=[
            pltpu.VMEM((4, Q, 2 * Q), F32),
            pltpu.VMEM((Q, 2 * Q), F32),
            pltpu.VMEM((Q, 2 * Q), F32),
            pltpu.VMEM((2, Q, Q), F32),
            pltpu.VMEM((2 * Q, Q), F32),
            pltpu.SemaphoreType.DMA((5,)),
        ],
        name="final",
    )(
        role, inv_own, inv_far, zt, mine_far[Q:], mine_far_peer[Q:], inv0, b, gt, inv1,
        d_part, d_far, *ring, *ring_peer,
    )
    return out[None]


def solution(mesh):
    in_specs = (P("box", None, "col"), P("box", None, None))
    out_specs = P("box", None, "col")
    return jax.shard_map(shards, mesh=mesh, in_specs=in_specs, out_specs=out_specs, check_vma=False)
```

```python
import jax
import jax.numpy as jnp
from jax import lax
from jax.experimental import pallas as pl
from jax.experimental.pallas import tpu as pltpu
from jax.sharding import PartitionSpec as P


Q = 256
F32 = jnp.float32
BF16 = jnp.bfloat16
HIGHEST = lax.Precision.HIGHEST
VMEM = pl.BlockSpec(memory_space=pltpu.VMEM)
SMEM = pl.BlockSpec(memory_space=pltpu.SMEM)
ANY = pl.BlockSpec(memory_space=pl.ANY)


def dot(a, b):
    return jnp.dot(a, b, precision=HIGHEST, preferred_element_type=F32)


def dot_t(a, b):
    return lax.dot_general(
        a, b, (((1,), (1,)), ((), ())), precision=HIGHEST, preferred_element_type=F32
    )


def split(x):
    high = x.astype(BF16)
    return high, (x - high.astype(F32)).astype(BF16)


def dot3(a, b, b_dim=0):
    (a1, a2), (b1, b2) = split(a), split(b)

    def mul(p, q):
        return lax.dot_general(p, q, (((1,), (b_dim,)), ((), ())), preferred_element_type=F32)

    return mul(a1, b1) + (mul(a1, b2) + mul(a2, b1))


def row_of(x, j):
    return jnp.broadcast_to(x[j : j + 1, :], (8, 128))


def col_of(x, j):
    return jnp.broadcast_to(x[:, j : j + 1], (8, 128))


def eliminate(rows, tile, base, lane, sub):
    cols = [col_of(rows[tile], base + j) for j in range(8)]
    rows = list(rows)
    for j in range(0, 8, 2):
        c0, c1 = cols[j], cols[j + 1]
        a, b2 = row_of(c0, j), row_of(c1, j)
        b, c = row_of(c0, j + 1), row_of(c1, j + 1)
        rd = 1.0 / (a * c - b * b2)
        l0, l1 = lane == base + j, lane == base + j + 1
        s0, s1 = sub == j, sub == j + 1

        def scaled(x):
            r0, r1 = row_of(x, j), row_of(x, j + 1)
            return (c * r0 - b2 * r1) * rd, (a * r1 - b * r0) * rd

        def put(old, n0, n1):
            return jnp.where(s0, n0, jnp.where(s1, n1, old - (c0 * n0 + c1 * n1)))

        for m in range(j + 2, 8):
            cols[m] = put(cols[m], *scaled(cols[m]))
        for i in range(len(rows)):
            n0, n1 = scaled(rows[i])
            old = rows[i]
            if i == tile:
                n0 = jnp.where(l0, c * rd, jnp.where(l1, -(b2 * rd), n0))
                n1 = jnp.where(l0, -(b * rd), jnp.where(l1, a * rd, n1))
                old = jnp.where(l0 | l1, 0.0, old)
            rows[i] = put(old, n0, n1)
    return rows


def update(rows, pivots, tile, base, in_block):
    cols = [col_of(rows[tile], base + j) for j in range(8)]
    out = []
    for i in range(len(rows)):
        x = jnp.where(in_block, 0.0, rows[i]) if i == tile else rows[i]
        p = [cols[j] * pivots[i][j] for j in range(8)]
        out.append(x - (((p[0] + p[1]) + (p[2] + p[3])) + ((p[4] + p[5]) + (p[6] + p[7]))))
    return out


def invert(A, w=32):
    n = A.shape[0]
    x = A[...]
    on_diagonal = lax.broadcasted_iota(jnp.int32, (n, n), 0) == lax.broadcasted_iota(jnp.int32, (n, n), 1)
    across = lax.rsqrt(jnp.sum(jnp.where(on_diagonal, x, 0.0), axis=0, keepdims=True))
    down = jnp.broadcast_to(across, (8, n)).T[:, 0:1]
    A[...] = x * down * across
    eliminate_all(A, w)
    A[...] = A[...] * down * across


def eliminate_all(A, w):
    n = A.shape[0]
    tiles, groups_in = n // 128, w // 8
    lane = lax.broadcasted_iota(jnp.int32, (8, 128), 1)
    sub = lax.broadcasted_iota(jnp.int32, (8, 128), 0)
    wide = lax.broadcasted_iota(jnp.int32, (1, n), 1)
    panel = A[0:w, :]
    for r0 in range(0, n, w):
        tile, b0 = r0 // 128, r0 % 128
        groups = [
            [panel[g * 8 : g * 8 + 8, i * 128 : i * 128 + 128] for i in range(tiles)]
            for g in range(groups_in)
        ]
        for b in range(groups_in):
            base = b0 + b * 8
            in_block = (lane >= base) & (lane < base + 8)
            done = eliminate(groups[b], tile, base, lane, sub)
            pivots = [[row_of(done[i], j) for j in range(8)] for i in range(tiles)]
            groups[b] = done
            for g in list(range(b + 1, groups_in)) + list(range(b)):
                groups[g] = update(groups[g], pivots, tile, base, in_block)
        final = jnp.concatenate([jnp.concatenate(g, axis=1) for g in groups], axis=0)
        in_panel = (wide >= r0) & (wide < r0 + w)

        def trail(lo, hi):
            x = A[lo:hi, :]
            return jnp.where(in_panel, 0.0, x) - dot(x[:, r0 : r0 + w], final)

        nxt = r0 + w
        if nxt < n:
            panel = trail(nxt, nxt + w)
            if nxt + w < n:
                A[nxt + w : n, :] = trail(nxt + w, n)
        if r0 > 0:
            A[0:r0, :] = trail(0, r0)
        A[r0:nxt, :] = final


def call(kernel, out_shape, in_specs, flops, scratch=(), limit=None):
    outs = [jax.ShapeDtypeStruct(s, F32) for s in out_shape]
    return pl.pallas_call(
        kernel,
        out_shape=outs,
        in_specs=in_specs,
        out_specs=[VMEM] * len(outs),
        scratch_shapes=list(scratch),
        cost_estimate=pl.CostEstimate(flops=flops, bytes_accessed=1 << 20, transcendentals=0),
        compiler_params=pltpu.CompilerParams(vmem_limit_bytes=limit or (40 << 20)),
    )


def one_hot(table, k):
    lanes = lax.broadcasted_iota(jnp.int32, (Q, Q), 1)
    return jnp.where(lanes == jnp.broadcast_to(table[:, k : k + 1], (Q, Q)), 1.0, 0.0).astype(BF16)


def picked(nodes, sides):
    picks = [nodes[pl.ds(s, 1), :] for s in sides]
    return jnp.concatenate(picks + [jnp.zeros((8 - len(sides), Q), jnp.int32)], axis=0).T


def mul(a, b):
    return jnp.dot(a, b, preferred_element_type=F32)


def mul_t(a, b):
    return lax.dot_general(a, b, (((1,), (1,)), ((), ())), preferred_element_type=F32)


def pieces(x):
    x1 = x.astype(BF16)
    rest = x - x1.astype(F32)
    x2 = rest.astype(BF16)
    return x1, x2, (rest - x2.astype(F32)).astype(BF16)


def permute_kernel(role, panel, nodes, u_out, d_out):
    sides = [role[1], role[2], role[3], role[4]]
    table = picked(nodes, sides + [role[0]])
    to_own = one_hot(table, 4)
    for k in range(4):
        hot = one_hot(table, k)
        x = panel[pl.ds(pl.multiple_of(sides[k] * Q, Q), Q), :]
        parts = [mul(hot, piece).astype(BF16) for piece in pieces(x)]
        if k < 2:
            moved = [mul_t(to_own, piece) for piece in parts]
        else:
            moved = [mul_t(piece, to_own) for piece in parts]
        to = u_out if k < 2 else d_out
        to[:, k % 2 * Q : k % 2 * Q + Q] = moved[0] + (moved[1] + moved[2])


def reorder(x, rows, cols):
    parts = [mul_t(mul(rows, piece).astype(BF16), cols) for piece in pieces(x)]
    return parts[0] + (parts[1] + parts[2])


def coupling_kernel(role, raw, g1, g2, g3, nodes, out):
    hot = one_hot(picked(nodes, [role[1]]), 0)
    out[...] = reorder(jnp.where(role[0] == role[1], raw[...], g1[...] + (g2[...] + g3[...])), hot, hot)


def inner_kernel(role, raw, g1, g2, g3, nodes, out):
    table = picked(nodes, [role[1], role[2]])
    hot_a, hot_c = one_hot(table, 0), one_hot(table, 1)

    def block(side):
        shift = (role[0] - side + 4) % 4
        a = jnp.where(shift == 0, raw[...], g1[...])
        b = jnp.where(shift == 2, g2[...], g3[...])
        return jnp.where(shift < 2, a, b)

    out[:, :Q] = reorder(block(role[1]), hot_c, hot_a)
    out[:, Q:] = reorder(block(role[2]), hot_c, hot_c)


def first_inverse_kernel(s_own, s_peer, inv):
    inv[...] = s_own[...] + s_peer[...]
    invert(inv)


def level_one_kernel(role, inv, own, peer, zt, c00, mine, c01, c11):
    west = role[5] == 0
    a, b = own[...], peer[...]
    kn_w, kn_e = jnp.where(west, a, b), jnp.where(west, b, a)
    k_w, n_w, k_e, n_e = kn_w[:, :Q], kn_w[:, Q:], kn_e[:, :Q], kn_e[:, Q:]
    z_w, z_e = dot(k_w, inv[...]), dot(k_e, inv[...])
    zt[:Q, :] = z_w
    zt[Q:, :] = z_e
    c00[...] = n_w - dot_t(z_w, k_w)
    we = -dot_t(z_w, k_e)
    ee = n_e - dot_t(z_e, k_e)
    c01[...] = we
    c11[...] = ee
    mine[:Q, :] = jnp.where(west, we, ee)
    mine[Q:, :] = jnp.where(west, z_w, z_e)


def second_inverse_kernel(c_own, c_peer, inv):
    inv[...] = c_own[...] + c_peer[...]
    invert(inv)


def third_inverse_kernel(role, inv0, c01, c11, far, far_peer, gt, b_out, inv):
    west = role[5] == 0
    f, g = far[:Q, :], far_peer[:Q, :]
    b = c01[...] + jnp.where(west, f, g)
    d = c11[...] + jnp.where(west, g, f)
    b_out[...] = b
    gt[...] = dot(b.T, inv0[...])
    inv[...] = d - dot(gt[...], b)
    invert(inv)


def final_kernel(
    role, table, inv_own, from_ext, zt_own, zt_far, zt_far_peer, inv0, b, gt, inv1,
    d_own, e_own, r0, r1, r2, swapped, out, ux, up, dp, iv, x, t, zf, sem,
):
    own, core, zpos, ext = role[0], role[5], role[6], role[7]
    half = 1 - ext
    even = 1 - own % 2
    near, far = (1 - ext) * (1 - even), (1 - ext) * even
    held = (r0, r1, r2, e_own) + tuple(swapped.at[pl.ds(k * Q, Q), :] for k in range(3))
    entry = ((zpos * 2 + core) * 4 + own) * 5
    for j in range(5):
        which = table[entry + j]
        to = up if j == 4 else ux.at[j]
        for i in range(3 if j == 4 else 0, 7):
            @pl.when(which == i)
            def _(i=i, j=j, to=to):
                pltpu.make_async_copy(held[i], to, sem.at[j]).start()
    for use, refs in (
        (ext == 1, (d_own.at[:, pl.ds(0, Q)], d_own.at[:, pl.ds(Q, Q)])),
        (far == 1, (from_ext.at[pl.ds(Q, Q), :], from_ext.at[pl.ds(2 * Q, Q), :])),
        (near == 1, (swapped.at[pl.ds(3 * Q, Q), pl.ds(0, Q)], swapped.at[pl.ds(3 * Q, Q), pl.ds(Q, Q)])),
    ):
        @pl.when(use)
        def _(refs=refs):
            for k in range(2):
                pltpu.make_async_copy(refs[k], dp.at[k], sem.at[5 + k]).start()
    i_copy = pltpu.make_async_copy(from_ext.at[pl.ds(0, Q), :], iv, sem.at[7])
    i_copy.start()
    p_copy = pltpu.make_async_copy(held[3], up, sem.at[4])
    west = core == 0
    zf[:Q, :] = jnp.where(west, zt_far[Q:, :], zt_far_peer[Q:, :])
    zf[Q:, :] = jnp.where(west, zt_far_peer[Q:, :], zt_far[Q:, :])
    p_copy.wait()
    i_copy.wait()
    is_far = far == 1
    a_p, c_p = up[:, :Q], up[:, Q:]
    inv_p = jnp.where(is_far, iv[...], inv_own[...])
    zt_p = jnp.where(is_far, zf[...], zt_own[...])
    p_core = jnp.where(near == 1, 1 - core, core)
    p_zpos = jnp.where(is_far, 1 - zpos, zpos)
    y = dot(a_p, inv_p)
    v2 = -dot_t(a_p, zt_p)
    on_west = p_core == 0
    v2_w = v2[:, :Q] + jnp.where(on_west, c_p, 0.0)
    v2_e = v2[:, Q:] + jnp.where(on_west, 0.0, c_p)
    u1 = dot(v2_w, inv0[...])
    s2 = dot(v2_e - dot(u1, b[...]), inv1[...])
    s1 = u1 - dot(s2, gt[...])
    x[:, :Q] = s1
    x[:, Q:] = s2
    xs = x[...]
    own_t = dot3(xs, zt_own[...])
    far_t = dot3(xs, zf[...])
    t[0] = jnp.where(is_far, -own_t, y - own_t)
    t[1] = jnp.where(is_far, y - far_t, -far_t)
    for j in range(4):
        pltpu.make_async_copy(held[3], ux.at[j], sem.at[j]).wait()
    pairs = ((0, 1), (0, 1), (0, 0), (1, 1))
    leaves = ((0, 0), (1, 1), (1, 0), (1, 0))
    for k in range(4):
        pair = jnp.where(half == 0, pairs[k][0], pairs[k][1])
        leaf = jnp.where(half == 0, leaves[k][0], leaves[k][1])
        tk = t[jnp.where(pair == zpos, 0, 1)]
        xk = jnp.where(leaf == 0, x[:, :Q], x[:, Q:])
        out[k * Q : k * Q + Q, :] = -(dot3(ux[k, :, :Q], tk, 1) + dot3(ux[k, :, Q:], xk, 1))
    z_row = pl.ds(pl.multiple_of(p_core * Q, Q), Q)
    x_row = pl.ds(pl.multiple_of((2 + p_zpos) * Q, Q), Q)
    for k in range(2):
        pltpu.make_async_copy(d_own.at[:, pl.ds(0, Q)], dp.at[k], sem.at[5 + k]).wait()

    @pl.when(half == 1 - p_core)
    def _():
        out[x_row, :] = out[x_row, :] + dp[0]

    @pl.when(half == p_zpos)
    def _():
        out[z_row, :] = out[z_row, :] + dp[1]


def sides_of(core, zpos):
    return 1 + 2 * core, 2 - 2 * zpos, 3 - 2 * core, 2 * zpos


def pairs_of(boxes, route):
    out = []
    for k in range(boxes // 4):
        for z in range(2):
            for core in range(2):
                for col in range(4):
                    to = route(core, z, col)
                    if to is not None:
                        out.append((
                            (4 * k + 2 * z + core) * 4 + col,
                            (4 * k + 2 * to[1] + to[0]) * 4 + to[2],
                        ))
    return out


def slot_of(core, zpos, col):
    return (core, 1 - (zpos ^ core), core, zpos ^ core)[col]


def plan_rounds():
    devices = [(core, z, col) for z in range(2) for core in range(2) for col in range(4)]
    half = {d: 0 if d[2] in sides_of(d[0], d[1])[2:] else 1 for d in devices}
    edges = []
    for d in devices:
        core, z, col = d
        for c in (2 * half[d], 2 * half[d] + 1):
            for k in range(2):
                if c != col and (col % 2 == 1 or k == core):
                    source = [s for s in devices if s[1] == z and s[2] == c and slot_of(*s) == k][0]
                    early = col % 2 == 0
                    if col % 2 == 1 and col // 2 != half[d] and (c, k) == (2 * half[d] + 1, 1):
                        edges.append((source, (1 - core, z, col), (c, k), 2))
                    else:
                        edges.append((source, d, (c, k), 2 if early else 3))
    edges.sort(key=lambda e: (e[3], e))
    sends, takes = {}, {}

    def place(n):
        if n == len(edges):
            return True
        source, to, panel, limit = edges[n]
        for r in range(limit):
            if (source, r) not in sends and (to, r) not in takes:
                sends[source, r] = to
                takes[to, r] = panel
                if place(n + 1):
                    return True
                del sends[source, r], takes[to, r]
        return False

    assert place(0)
    routes = [{a: b for (a, r), b in sends.items() if r == q} for q in range(3)]
    table = []
    for d in devices:
        core, z, col = d
        sibling = (1 - core, z, col)
        for c in (2 * half[d], 2 * half[d] + 1):
            for k in range(2):
                if c == col:
                    table.append(3 if k == slot_of(*d) else 4)
                    continue
                here = [r for r in range(3) if takes.get((d, r)) == (c, k)]
                there = [5 + r for r in range(2) if takes.get((sibling, r)) == (c, k)]
                table.append((here + there)[0])
        table.append(4 if half[d] == 1 and col % 2 == 1 else 3)
    return routes, table


def body(leaf_maps, leaf_nodes):
    boxes = lax.axis_size("box")

    def send(value, route):
        return lax.ppermute(value, ("box", "col"), pairs_of(boxes, route))

    def swap_core(core, z, col):
        return 1 - core, z, col

    def swap_z(core, z, col):
        return core, 1 - z, col

    def is_ext(core, z, col):
        return col in sides_of(core, z)[2:]

    def shift_if(test, step):
        return lambda core, z, col: (core, z, (col + step) % 4) if test(core, z, col) else None

    box = lax.axis_index("box")
    col = lax.axis_index("col")
    core, zpos = box % 2, box // 2 % 2
    ia, ic, ex, ez = sides_of(core, zpos)
    ext = ((col == ex) | (col == ez)).astype(jnp.int32)
    role = jnp.stack([col, ia, ic, ex, ez, core, zpos, ext]).astype(jnp.int32)
    routes, table = plan_rounds()

    square = (Q, Q)
    panel, nodes = leaf_maps[0], leaf_nodes[0]

    def from_ia(core, z, col):
        return col == sides_of(core, z)[0]

    raw = lax.dynamic_slice(panel, (ia * Q, 0), square)
    got = [send(raw, shift_if(from_ia, s)) for s in (1, 2, 3)]
    u_part, d_part = call(permute_kernel, [(Q, 2 * Q)] * 2, [SMEM, VMEM, VMEM], 1 << 30)(role, panel, nodes)
    s_own, = call(coupling_kernel, [square], [SMEM] + [VMEM] * 5, 1 << 28)(role, raw, *got, nodes)
    s_peer = send(s_own, swap_core)

    def from_inner(core, z, col):
        return col in sides_of(core, z)[:2]

    raw = lax.dynamic_slice(panel, (ic * Q, 0), square)
    inner = [raw] + [send(raw, shift_if(from_inner, s)) for s in (1, 2, 3)]

    def spread(core, z, col):
        if not is_ext(core, z, col):
            return None
        return (core, 1 - z, col) if col % 2 == 0 else (1 - core, 1 - z, col)

    e_own = jnp.where(ext == 1, u_part, send(u_part, spread))

    def to_far_inner(core, z, col):
        return (core, 1 - z, col) if is_ext(core, z, col) and col % 2 == 0 else None

    inv_own, = call(first_inverse_kernel, [square], [VMEM] * 2, 10 << 30)(s_own, s_peer)

    kn_own, = call(inner_kernel, [(Q, 2 * Q)], [SMEM] + [VMEM] * 5, 1 << 28)(role, *inner, nodes)
    kn_peer = send(kn_own, swap_core)
    rounds = [send(e_own, lambda *d, r=r: routes[r].get(d)) for r in range(3)]
    swapped = send(jnp.concatenate([e_own, rounds[0], rounds[1], d_part], axis=0), swap_core)

    zt, c00, mine, c01, c11 = call(
        level_one_kernel, [(2 * Q, Q), square, (2 * Q, Q), square, square], [SMEM] + [VMEM] * 3, 2 << 30
    )(role, inv_own, kn_own, kn_peer)

    c00_far = send(c00, swap_z)
    mine_far = send(mine, swap_z)
    mine_far_peer = send(mine_far, swap_core)

    to_far = jnp.concatenate([inv_own, d_part[:, :Q], d_part[:, Q:]], axis=0)
    from_ext = send(to_far, to_far_inner)

    inv0, = call(second_inverse_kernel, [square], [VMEM] * 2, 10 << 30)(c00, c00_far)
    gt, b, inv1 = call(
        third_inverse_kernel, [square] * 3, [SMEM] + [VMEM] * 5, 10 << 30
    )(role, inv0, c01, c11, mine_far, mine_far_peer)
    out, = call(
        final_kernel,
        [(4 * Q, Q)],
        [SMEM] * 2 + [VMEM, ANY] + [VMEM] * 7 + [ANY] * 6,
        4 << 30,
        scratch=[
            pltpu.VMEM((4, Q, 2 * Q), F32),
            pltpu.VMEM((Q, 2 * Q), F32),
            pltpu.VMEM((2, Q, Q), F32),
            pltpu.VMEM((Q, Q), F32),
            pltpu.VMEM((Q, 2 * Q), F32),
            pltpu.VMEM((2, Q, Q), F32),
            pltpu.VMEM((2 * Q, Q), F32),
            pltpu.SemaphoreType.DMA((8,)),
        ],
    )(
        role, jnp.asarray(table, dtype=jnp.int32), inv_own, from_ext, zt, mine_far, mine_far_peer, inv0, b, gt,
        inv1, d_part, e_own, *rounds, swapped,
    )
    return out[None]


def solution(mesh):
    in_specs = (P("box", None, "col"), P("box", None, None))
    out_specs = P("box", None, "col")
    return jax.shard_map(body, mesh=mesh, in_specs=in_specs, out_specs=out_specs, check_vma=False)
```

```python
import jax
import jax.numpy as jnp
from jax import lax
from jax.experimental import pallas as pl
from jax.experimental.pallas import tpu as pltpu
from jax.sharding import PartitionSpec as P


Q = 256
F32 = jnp.float32
BF16 = jnp.bfloat16
HIGHEST = lax.Precision.HIGHEST
VMEM = pl.BlockSpec(memory_space=pltpu.VMEM)
SMEM = pl.BlockSpec(memory_space=pltpu.SMEM)
ANY = pl.BlockSpec(memory_space=pl.ANY)


def dot(a, b):
    return jnp.dot(a, b, precision=HIGHEST, preferred_element_type=F32)


def dot_t(a, b):
    return lax.dot_general(
        a, b, (((1,), (1,)), ((), ())), precision=HIGHEST, preferred_element_type=F32
    )


def split(x):
    high = x.astype(BF16)
    return high, (x - high.astype(F32)).astype(BF16)


def dot3(a, b, b_dim=0):
    (a1, a2), (b1, b2) = split(a), split(b)

    def mul(p, q):
        return lax.dot_general(p, q, (((1,), (b_dim,)), ((), ())), preferred_element_type=F32)

    return mul(a1, b1) + (mul(a1, b2) + mul(a2, b1))


def row_of(x, j):
    return jnp.broadcast_to(x[j : j + 1, :], (8, 128))


def col_of(x, j):
    return jnp.broadcast_to(x[:, j : j + 1], (8, 128))


def eliminate(rows, tile, base, lane, sub):
    cols = [col_of(rows[tile], base + j) for j in range(8)]
    rows = list(rows)
    for j in range(0, 8, 2):
        c0, c1 = cols[j], cols[j + 1]
        a, b2 = row_of(c0, j), row_of(c1, j)
        b, c = row_of(c0, j + 1), row_of(c1, j + 1)
        rd = 1.0 / (a * c - b * b2)
        l0, l1 = lane == base + j, lane == base + j + 1
        s0, s1 = sub == j, sub == j + 1

        def scaled(x):
            r0, r1 = row_of(x, j), row_of(x, j + 1)
            return (c * r0 - b2 * r1) * rd, (a * r1 - b * r0) * rd

        def put(old, n0, n1):
            return jnp.where(s0, n0, jnp.where(s1, n1, old - (c0 * n0 + c1 * n1)))

        for m in range(j + 2, 8):
            cols[m] = put(cols[m], *scaled(cols[m]))
        for i in range(len(rows)):
            n0, n1 = scaled(rows[i])
            old = rows[i]
            if i == tile:
                n0 = jnp.where(l0, c * rd, jnp.where(l1, -(b2 * rd), n0))
                n1 = jnp.where(l0, -(b * rd), jnp.where(l1, a * rd, n1))
                old = jnp.where(l0 | l1, 0.0, old)
            rows[i] = put(old, n0, n1)
    return rows


def update(rows, pivots, tile, base, in_block):
    cols = [col_of(rows[tile], base + j) for j in range(8)]
    out = []
    for i in range(len(rows)):
        x = jnp.where(in_block, 0.0, rows[i]) if i == tile else rows[i]
        p = [cols[j] * pivots[i][j] for j in range(8)]
        out.append(x - (((p[0] + p[1]) + (p[2] + p[3])) + ((p[4] + p[5]) + (p[6] + p[7]))))
    return out


def invert(A, w=32):
    n = A.shape[0]
    x = A[...]
    on_diagonal = lax.broadcasted_iota(jnp.int32, (n, n), 0) == lax.broadcasted_iota(jnp.int32, (n, n), 1)
    across = lax.rsqrt(jnp.sum(jnp.where(on_diagonal, x, 0.0), axis=0, keepdims=True))
    down = jnp.broadcast_to(across, (8, n)).T[:, 0:1]
    A[...] = x * down * across
    eliminate_all(A, w)
    A[...] = A[...] * down * across


def eliminate_all(A, w):
    n = A.shape[0]
    tiles, groups_in = n // 128, w // 8
    lane = lax.broadcasted_iota(jnp.int32, (8, 128), 1)
    sub = lax.broadcasted_iota(jnp.int32, (8, 128), 0)
    wide = lax.broadcasted_iota(jnp.int32, (1, n), 1)
    panel = A[0:w, :]
    for r0 in range(0, n, w):
        tile, b0 = r0 // 128, r0 % 128
        groups = [
            [panel[g * 8 : g * 8 + 8, i * 128 : i * 128 + 128] for i in range(tiles)]
            for g in range(groups_in)
        ]
        for b in range(groups_in):
            base = b0 + b * 8
            in_block = (lane >= base) & (lane < base + 8)
            done = eliminate(groups[b], tile, base, lane, sub)
            pivots = [[row_of(done[i], j) for j in range(8)] for i in range(tiles)]
            groups[b] = done
            for g in list(range(b + 1, groups_in)) + list(range(b)):
                groups[g] = update(groups[g], pivots, tile, base, in_block)
        final = jnp.concatenate([jnp.concatenate(g, axis=1) for g in groups], axis=0)
        in_panel = (wide >= r0) & (wide < r0 + w)

        def trail(lo, hi):
            x = A[lo:hi, :]
            return jnp.where(in_panel, 0.0, x) - dot(x[:, r0 : r0 + w], final)

        nxt = r0 + w
        if nxt < n:
            panel = trail(nxt, nxt + w)
            if nxt + w < n:
                A[nxt + w : n, :] = trail(nxt + w, n)
        if r0 > 0:
            A[0:r0, :] = trail(0, r0)
        A[r0:nxt, :] = final


def call(kernel, out_shape, in_specs, flops, scratch=(), limit=None):
    outs = [jax.ShapeDtypeStruct(s, F32) for s in out_shape]
    return pl.pallas_call(
        kernel,
        out_shape=outs,
        in_specs=in_specs,
        out_specs=[VMEM] * len(outs),
        scratch_shapes=list(scratch),
        cost_estimate=pl.CostEstimate(flops=flops, bytes_accessed=1 << 20, transcendentals=0),
        compiler_params=pltpu.CompilerParams(vmem_limit_bytes=limit or (40 << 20)),
    )


def one_hot(table, k):
    lanes = lax.broadcasted_iota(jnp.int32, (Q, Q), 1)
    return jnp.where(lanes == jnp.broadcast_to(table[:, k : k + 1], (Q, Q)), 1.0, 0.0).astype(BF16)


def picked(nodes, sides):
    picks = [nodes[pl.ds(s, 1), :] for s in sides]
    return jnp.concatenate(picks + [jnp.zeros((8 - len(sides), Q), jnp.int32)], axis=0).T


def mul(a, b):
    return jnp.dot(a, b, preferred_element_type=F32)


def mul_t(a, b):
    return lax.dot_general(a, b, (((1,), (1,)), ((), ())), preferred_element_type=F32)


def pieces(x):
    x1 = x.astype(BF16)
    rest = x - x1.astype(F32)
    x2 = rest.astype(BF16)
    return x1, x2, (rest - x2.astype(F32)).astype(BF16)


def permute_kernel(role, panel, nodes, u_out, d_out):
    sides = [role[1], role[2], role[3], role[4]]
    table = picked(nodes, sides + [role[0]])
    to_own = one_hot(table, 4)
    for k in range(4):
        hot = one_hot(table, k)
        x = panel[pl.ds(pl.multiple_of(sides[k] * Q, Q), Q), :]
        parts = [mul(hot, piece).astype(BF16) for piece in pieces(x)]
        if k < 2:
            moved = [mul_t(to_own, piece) for piece in parts]
        else:
            moved = [mul_t(piece, to_own) for piece in parts]
        to = u_out if k < 2 else d_out
        to[:, k % 2 * Q : k % 2 * Q + Q] = moved[0] + (moved[1] + moved[2])


def reorder(x, rows, cols):
    parts = [mul_t(mul(rows, piece).astype(BF16), cols) for piece in pieces(x)]
    return parts[0] + (parts[1] + parts[2])


def coupling_kernel(role, raw, g1, g2, g3, nodes, out):
    hot = one_hot(picked(nodes, [role[1]]), 0)
    out[...] = reorder(jnp.where(role[0] == role[1], raw[...], g1[...] + (g2[...] + g3[...])), hot, hot)


def inner_kernel(role, raw, g1, g2, g3, nodes, out):
    table = picked(nodes, [role[1], role[2]])
    hot_a, hot_c = one_hot(table, 0), one_hot(table, 1)

    def block(side):
        shift = (role[0] - side + 4) % 4
        a = jnp.where(shift == 0, raw[...], g1[...])
        b = jnp.where(shift == 2, g2[...], g3[...])
        return jnp.where(shift < 2, a, b)

    out[:, :Q] = reorder(block(role[1]), hot_c, hot_a)
    out[:, Q:] = reorder(block(role[2]), hot_c, hot_c)


def first_inverse_kernel(s_own, s_peer, inv):
    inv[...] = s_own[...] + s_peer[...]
    invert(inv)


def level_one_kernel(role, inv, own, peer, zt, c00, c00_half, mine, c01, c11):
    west = role[5] == 0
    a, b = own[...], peer[...]
    kn_w, kn_e = jnp.where(west, a, b), jnp.where(west, b, a)
    k_w, n_w, k_e, n_e = kn_w[:, :Q], kn_w[:, Q:], kn_e[:, :Q], kn_e[:, Q:]
    z_w, z_e = dot(k_w, inv[...]), dot(k_e, inv[...])
    zt[:Q, :] = z_w
    zt[Q:, :] = z_e
    ww = n_w - dot_t(z_w, k_w)
    c00[...] = ww
    c00_half[...] = jnp.where(west, ww[: Q // 2], ww[Q // 2 :])
    we = -dot_t(z_w, k_e)
    ee = n_e - dot_t(z_e, k_e)
    c01[...] = we
    c11[...] = ee
    mine[:Q, :] = jnp.where(west, we, ee)
    mine[Q:, :] = jnp.where(west, z_w, z_e)


def second_inverse_kernel(role, c_own, far, far_peer, inv):
    west = role[5] == 0
    f, g = far[...], far_peer[...]
    inv[: Q // 2, :] = c_own[: Q // 2, :] + jnp.where(west, f, g)
    inv[Q // 2 :, :] = c_own[Q // 2 :, :] + jnp.where(west, g, f)
    invert(inv)


def third_inverse_kernel(role, inv0, c01, c11, far, far_peer, gt, b_out, inv):
    west = role[5] == 0
    f, g = far[:Q, :], far_peer[:Q, :]
    b = c01[...] + jnp.where(west, f, g)
    d = c11[...] + jnp.where(west, g, f)
    b_out[...] = b
    gt[...] = dot(b.T, inv0[...])
    inv[...] = d - dot(gt[...], b)
    invert(inv)


def final_kernel(
    role, table, inv_own, inv_far, zt_own, zt_far, zt_far_peer, inv0, b, gt, inv1,
    d_own, d_far, e_own, r0, r1, r2, swapped, out, ux, up, dp, x, t, zf, sem,
):
    own, core, zpos, ext = role[0], role[5], role[6], role[7]
    half = 1 - ext
    even = 1 - own % 2
    near, far = (1 - ext) * (1 - even), (1 - ext) * even
    held = (r0, r1, r2, e_own) + tuple(swapped.at[pl.ds(k * Q, Q), :] for k in range(4))
    entry = ((zpos * 2 + core) * 4 + own) * 5
    for j in range(5):
        which = table[entry + j]
        to = up if j == 4 else ux.at[j]
        for i in range(3 if j == 4 else 0, 8):
            @pl.when(which == i)
            def _(i=i, j=j, to=to):
                pltpu.make_async_copy(held[i], to, sem.at[j]).start()
    for use, ref in ((ext == 1, d_own), (ext == 0, d_far)):
        @pl.when(use)
        def _(ref=ref):
            for k in range(2):
                pltpu.make_async_copy(ref.at[:, pl.ds(k * Q, Q)], dp.at[k], sem.at[5 + k]).start()
    p_copy = pltpu.make_async_copy(held[3], up, sem.at[4])
    west = core == 0
    zf[:Q, :] = jnp.where(west, zt_far[Q:, :], zt_far_peer[Q:, :])
    zf[Q:, :] = jnp.where(west, zt_far_peer[Q:, :], zt_far[Q:, :])
    p_copy.wait()
    is_far = far == 1
    a_p, c_p = up[:, :Q], up[:, Q:]
    inv_p = jnp.where(is_far, inv_far[...], inv_own[...])
    zt_p = jnp.where(is_far, zf[...], zt_own[...])
    p_core = jnp.where(near == 1, 1 - core, core)
    p_zpos = jnp.where(is_far, 1 - zpos, zpos)
    y = dot(a_p, inv_p)
    v2 = -dot_t(a_p, zt_p)
    on_west = p_core == 0
    v2_w = v2[:, :Q] + jnp.where(on_west, c_p, 0.0)
    v2_e = v2[:, Q:] + jnp.where(on_west, 0.0, c_p)
    u1 = dot(v2_w, inv0[...])
    s2 = dot(v2_e - dot(u1, b[...]), inv1[...])
    s1 = u1 - dot(s2, gt[...])
    x[:, :Q] = s1
    x[:, Q:] = s2
    xs = x[...]
    own_t = dot3(xs, zt_own[...])
    far_t = dot3(xs, zf[...])
    t[0] = jnp.where(is_far, -own_t, y - own_t)
    t[1] = jnp.where(is_far, y - far_t, -far_t)
    for j in range(4):
        pltpu.make_async_copy(held[3], ux.at[j], sem.at[j]).wait()
    pairs = ((0, 1), (0, 1), (0, 0), (1, 1))
    leaves = ((0, 0), (1, 1), (1, 0), (1, 0))
    for k in range(4):
        pair = jnp.where(half == 0, pairs[k][0], pairs[k][1])
        leaf = jnp.where(half == 0, leaves[k][0], leaves[k][1])
        tk = t[jnp.where(pair == zpos, 0, 1)]
        xk = jnp.where(leaf == 0, x[:, :Q], x[:, Q:])
        out[k * Q : k * Q + Q, :] = -(dot3(ux[k, :, :Q], tk, 1) + dot3(ux[k, :, Q:], xk, 1))
    z_row = pl.ds(pl.multiple_of(p_core * Q, Q), Q)
    x_row = pl.ds(pl.multiple_of((2 + p_zpos) * Q, Q), Q)
    for k in range(2):
        pltpu.make_async_copy(d_own.at[:, pl.ds(0, Q)], dp.at[k], sem.at[5 + k]).wait()

    @pl.when(half == 1 - p_core)
    def _():
        out[x_row, :] = out[x_row, :] + dp[0]

    @pl.when(half == p_zpos)
    def _():
        out[z_row, :] = out[z_row, :] + dp[1]


def sides_of(core, zpos):
    return 1 + 2 * core, 2 - 2 * zpos, 3 - 2 * core, 2 * zpos


def pairs_of(boxes, route):
    out = []
    for k in range(boxes // 4):
        for z in range(2):
            for core in range(2):
                for col in range(4):
                    to = route(core, z, col)
                    if to is not None:
                        out.append((
                            (4 * k + 2 * z + core) * 4 + col,
                            (4 * k + 2 * to[1] + to[0]) * 4 + to[2],
                        ))
    return out


def slot_of(core, zpos, col):
    return (core, 1 - (zpos ^ core), core, zpos ^ core)[col]


def panel_table():
    table = []
    for z in range(2):
        for core in range(2):
            for col in range(4):
                half = 0 if col in sides_of(core, z)[2:] else 1
                for c in (2 * half, 2 * half + 1):
                    for k in range(2):
                        mine = k == slot_of(core, z, c)
                        if c == col:
                            table.append(3 if mine else 4)
                        else:
                            swap = (col ^ 1, 3 - col, col ^ 2).index(c)
                            table.append(swap if mine else 5 + swap)
                table.append(4 if half == 1 and col % 2 == 1 else 3)
    return table


def body(leaf_maps, leaf_nodes):
    boxes = lax.axis_size("box")

    def send(value, route):
        return lax.ppermute(value, ("box", "col"), pairs_of(boxes, route))

    def swap_core(core, z, col):
        return 1 - core, z, col

    def swap_z(core, z, col):
        return core, 1 - z, col

    def shift_if(test, step):
        return lambda core, z, col: (core, z, (col + step) % 4) if test(core, z, col) else None

    box = lax.axis_index("box")
    col = lax.axis_index("col")
    core, zpos = box % 2, box // 2 % 2
    ia, ic, ex, ez = sides_of(core, zpos)
    ext = ((col == ex) | (col == ez)).astype(jnp.int32)
    role = jnp.stack([col, ia, ic, ex, ez, core, zpos, ext]).astype(jnp.int32)
    table = panel_table()

    square = (Q, Q)
    panel, nodes = leaf_maps[0], leaf_nodes[0]

    def from_ia(core, z, col):
        return col == sides_of(core, z)[0]

    raw = lax.dynamic_slice(panel, (ia * Q, 0), square)
    got = [send(raw, shift_if(from_ia, s)) for s in (1, 2, 3)]
    u_part, d_part = call(permute_kernel, [(Q, 2 * Q)] * 2, [SMEM, VMEM, VMEM], 1 << 30)(role, panel, nodes)
    s_own, = call(coupling_kernel, [square], [SMEM] + [VMEM] * 5, 1 << 28)(role, raw, *got, nodes)
    s_peer = send(s_own, swap_core)

    def from_inner(core, z, col):
        return col in sides_of(core, z)[:2]

    raw = lax.dynamic_slice(panel, (ic * Q, 0), square)
    inner = [raw] + [send(raw, shift_if(from_inner, s)) for s in (1, 2, 3)]

    def spread(core, z, col):
        return (core, 1 - z, col) if col % 2 == 0 else (1 - core, 1 - z, col)

    e_own = jnp.where(ext == 1, u_part, send(u_part, spread))

    def to_inner(core, z, col):
        return (core, 1 - z, col) if col % 2 == 0 else (1 - core, z, col)

    inv_own, = call(first_inverse_kernel, [square], [VMEM] * 2, 10 << 30)(s_own, s_peer)

    kn_own, = call(inner_kernel, [(Q, 2 * Q)], [SMEM] + [VMEM] * 5, 1 << 28)(role, *inner, nodes)
    kn_peer = send(kn_own, swap_core)
    swaps = (
        lambda core, z, col: (core, z, col ^ 1),
        lambda core, z, col: (core, z, 3 - col),
        lambda core, z, col: (1 - core, z, col) if z == 0 and col % 2 == 0 else (core, z, col ^ 2),
    )
    rounds = [send(e_own, route) for route in swaps]
    swapped = send(jnp.concatenate([e_own, *rounds], axis=0), swap_core)

    zt, c00, c00_half, mine, c01, c11 = call(
        level_one_kernel, [(2 * Q, Q), square, (Q // 2, Q), (2 * Q, Q), square, square], [SMEM] + [VMEM] * 3, 2 << 30
    )(role, inv_own, kn_own, kn_peer)

    c00_far = send(c00_half, swap_z)
    c00_far_peer = send(c00_far, swap_core)
    mine_far = send(mine, swap_z)
    mine_far_peer = send(mine_far, swap_core)

    d_far = send(d_part, to_inner)
    inv_far = send(inv_own, to_inner)

    inv0, = call(second_inverse_kernel, [square], [SMEM] + [VMEM] * 3, 10 << 30)(role, c00, c00_far, c00_far_peer)
    gt, b, inv1 = call(
        third_inverse_kernel, [square] * 3, [SMEM] + [VMEM] * 5, 10 << 30
    )(role, inv0, c01, c11, mine_far, mine_far_peer)
    out, = call(
        final_kernel,
        [(4 * Q, Q)],
        [SMEM] * 2 + [VMEM] * 9 + [ANY] * 7,
        4 << 30,
        scratch=[
            pltpu.VMEM((4, Q, 2 * Q), F32),
            pltpu.VMEM((Q, 2 * Q), F32),
            pltpu.VMEM((2, Q, Q), F32),
            pltpu.VMEM((Q, 2 * Q), F32),
            pltpu.VMEM((2, Q, Q), F32),
            pltpu.VMEM((2 * Q, Q), F32),
            pltpu.SemaphoreType.DMA((7,)),
        ],
    )(
        role, jnp.asarray(table, dtype=jnp.int32), inv_own, inv_far, zt, mine_far, mine_far_peer, inv0, b, gt,
        inv1, d_part, d_far, e_own, *rounds, swapped,
    )
    return out[None]


def solution(mesh):
    in_specs = (P("box", None, "col"), P("box", None, None))
    out_specs = P("box", None, "col")
    return jax.shard_map(body, mesh=mesh, in_specs=in_specs, out_specs=out_specs, check_vma=False)
```
